256 devices in a mesh: occ: 64 (over x, z, core), aux: 4 (over y).
Axes of the slice: x: 4, y: 4, z: 8, core: 2. Of those that a mesh axis runs over, the one named last changes fastest.
Arguments:
- factors: bfloat16 [128, 256, 1024], P('occ', None, 'aux'), may hold values from -0.8984375 to 0.8984375
- occ_energy: float32 [128], replicated, may hold values from -3 to -0.5
- vir_energy: float32 [256], replicated, may hold values from 0.5 to 3
- i_slot: int32 [2048], P('occ'), may hold values from 0 to 1
- j_slot: int32 [2048], P('occ'), may hold values from 0 to 1
- partner_device: int32 [2048, 1], P('occ'), may hold values from 0 to 63; in each aligned block of 32 rows (0 to 31, 32 to 63, ...) at most 2 rows name the same one
- pair_count: int32 [64], P('occ'), may hold values from 1 to 32, 1843 in all
Outputs:
- gamma: float32 [128, 256, 1024], P('occ', None, 'aux')
- aux_matrix: float32 [1024, 1024], P('aux', 'occ')
The draws below stay inside these ranges and needn't reach their ends.
Inputs may be any that keep to these rules, and one draw needn't show every extreme that they name: `partner_device`: among the 32 pair slots of one occ index, at most 2 name the same partner device, and some index reaches 2.
All inputs are finite; a program needn't handle non-finite values. No bound on the sum of `pair_count` on one device may be relied on, other than what follows from the above.
Results may differ from the reference program's by a relative error of at most 0.0013.
Values may be sent and summed in bfloat16 or wider, within the bound.
No kernel may reach another device: no remote copies, remote signals or barrier semaphores. Data moves between devices by JAX's collectives and lax.ppermute only.
A program may use at most 128 MiB of HBM per device.

```python
import math
import jax
import jax.numpy as jnp
import numpy as np
from jax import lax

V = 256
Q = 1024
OCC_DEV = 2
PAIR_DEV = 32
O = 128
PAIRS = 2048
CAP = 2
N_OCC = 64


def set_ends(result, rng, least, top_value):
    longest = result.shape.index(max(result.shape))
    spots = []
    for shift in (0, 1):
        where = [jax.random.randint(jax.random.fold_in(rng, axis), (), 0, length) for axis, length in enumerate(result.shape)]
        where[longest] = (where[longest] + shift) % result.shape[longest]
        spots.append(tuple(where))
    return result.at[spots[0]].set(least).at[spots[1]].set(top_value)


def level_of(stream_key, shape, shards, least, high):
    level = 1.0
    for axis_at, blocks in shards:
        draws = jax.random.uniform(jax.random.fold_in(jax.random.fold_in(stream_key, 6), axis_at), (blocks,), jnp.float32, least / len(shards), high / len(shards))
        level = level * jnp.repeat(jnp.exp(draws), shape[axis_at] // blocks).reshape((-1,) + (1,) * (len(shape) - 1 - axis_at))
    return level


def split_up(number_of, total, reach, slope):
    weights = [(1 << 20) // math.isqrt(standing ** slope) + 1 for standing in range(2, number_of + 1)]
    spare, holding = total - reach - (number_of - 1), [1] * (number_of - 1)
    while spare > 0:
        free = [i for i in range(number_of - 1) if holding[i] < reach]
        pool, budget = sum([weights[i] for i in free]), spare
        for i in free:
            more = min(reach - holding[i], max(1, budget * weights[i] // pool), spare)
            holding[i] = holding[i] + more
            spare = spare - more
    return np.array([reach] + holding)


def ragged_sizes(stream_key, amount, total, limit, slope):
    if amount == 2:
        one = jax.random.randint(stream_key, (), max(1, total - limit), min(limit, total - 1) + 1)
        return jnp.stack([one, total - one])
    lengths = jnp.asarray(split_up(amount, total, limit, slope), jnp.int32)
    couples = (amount - 1) // 2
    giver, receiver = lengths[1:1 + 2 * couples:2], lengths[2:2 + 2 * couples:2]
    margin = jnp.minimum(giver - 1, limit - receiver)
    moved = jax.random.randint(jax.random.fold_in(stream_key, 1), (couples,), 0, 1 << 20) % (margin + 1)
    lengths = lengths.at[1:1 + 2 * couples:2].set(giver - moved).at[2:2 + 2 * couples:2].set(receiver + moved)
    return lengths[jax.random.permutation(jax.random.fold_in(stream_key, 2), amount)]


def shared_out(own_key, own, number, rows, count, top, limit, lean):
    sequence = jax.random.permutation(own_key, count)
    packed, usual = shares(count, rows * top, limit, lean, True), shares(count, rows * top, limit, lean, False)
    places = jnp.arange(count)

    def named(lengths, turn):
        used = int((lengths > 0).sum())
        fixed = max(1, used // 4)
        passed = fixed + (places - fixed + turn * (used - fixed)) % max(1, count - fixed)
        return jnp.zeros((count,), jnp.int32).at[sequence[jnp.where(places < fixed, places, passed)]].set(jnp.asarray(lengths, jnp.int32))

    lengths = jnp.where(number % 4 == 0, named(packed, number // 4), named(usual, number - number // 4 - 1))
    mixed = jax.random.permutation(jax.random.fold_in(own, 3), count)
    source_of, receiver = mixed[0:count // 2 * 2:2], mixed[1:count // 2 * 2:2]
    room = jnp.minimum(lengths[source_of] - 1, limit - lengths[receiver]) // 2
    room = jnp.where((source_of == sequence[0]) | (receiver == sequence[0]) | (lengths[receiver] == 0), 0, jnp.maximum(room, 0))
    passed = jax.random.randint(jax.random.fold_in(own, 4), (count // 2,), 0, 1 << 20) % (room + 1)
    lengths = lengths.at[source_of].add(-passed).at[receiver].add(passed)
    items = jnp.searchsorted(jnp.cumsum(lengths), jnp.arange(rows * top), side="right").astype(jnp.int32)
    table = items.reshape(top, rows).T
    table = table[jax.random.permutation(jax.random.fold_in(own, 1), rows)]
    turn = jax.random.randint(jax.random.fold_in(own, 2), (rows, 1), 0, top)
    return jnp.take_along_axis(table, (jnp.arange(top)[None, :] + turn) % top, axis=1)


def shares(count, total, most, slope, full):
    loads = [(1 << 20) // math.isqrt(grade ** slope) + 1 for grade in range(1, count + 1)]
    largest = most if full else min(most, max(-(-total // count), total * loads[0] // sum(loads)))
    least = 1 if total - largest >= count - 1 else 0
    given, rest = [largest] + [least] * (count - 1), total - largest - least * (count - 1)
    while rest > 0:
        candidates = [i for i in range(1, count) if given[i] < largest] or [i for i in range(1, count) if given[i] < most]
        whole, remaining = sum([loads[i] for i in candidates]), rest
        for i in candidates:
            more = min(most - given[i], max(1, remaining * loads[i] // whole), rest)
            given[i] = given[i] + more
            rest = rest - more
    return np.array(given)


def gaussian(own_key, extent, scale, most, pieces=(), kind=jnp.bfloat16):
    values = scale * jax.random.normal(own_key, extent, jnp.float32)
    if pieces:
        values = values * level_of(own_key, extent, pieces, -0.22, 0.18)
    return jnp.clip(values, -most, most).astype(kind)


def setup_inputs(seed: int = 0) -> dict:
    arg_keys = jax.random.split(jax.random.key(seed), 8)
    factors = gaussian(arg_keys[0], (O, V, Q), 0.15, 0.8984375, ((0, 64), (2, 4)))
    occ_energy = jnp.clip(jax.random.uniform(arg_keys[1], (O,), jnp.float32, -3.0, -0.5), -3.0, -0.5)
    vir_energy = jnp.clip(jax.random.uniform(arg_keys[2], (V,), jnp.float32, 0.5, 3.0), 0.5, 3.0)
    i_slot = set_ends(jax.random.randint(arg_keys[3], (PAIRS,), 0, OCC_DEV), jax.random.fold_in(arg_keys[3], 1), 0, OCC_DEV - 1).astype(jnp.int32)
    j_slot = set_ends(jax.random.randint(arg_keys[4], (PAIRS,), 0, OCC_DEV), jax.random.fold_in(arg_keys[4], 1), 0, OCC_DEV - 1).astype(jnp.int32)
    partner_device_keys = jax.random.split(jax.random.fold_in(arg_keys[5], 1), PAIRS // PAIR_DEV)
    partner_device_turns = jax.random.permutation(jax.random.fold_in(arg_keys[5], 3), PAIRS // PAIR_DEV)
    partner_device = jax.vmap(lambda own, number: shared_out(jax.random.fold_in(arg_keys[5], 2), own, number, PAIR_DEV, N_OCC, 1, CAP, 2))(partner_device_keys, partner_device_turns).reshape((PAIRS, 1))
    pair_count = ragged_sizes(arg_keys[6], N_OCC, N_OCC * PAIR_DEV * 9 // 10, PAIR_DEV, 2).astype(jnp.int32)
    return dict(factors=factors, occ_energy=occ_energy, vir_energy=vir_energy, i_slot=i_slot, j_slot=j_slot, partner_device=partner_device, pair_count=pair_count)


def reference(factors, occ_energy, vir_energy, i_slot, j_slot, partner_device, pair_count):
    orbitals = OCC_DEV * N_OCC
    total_pairs = N_OCC * PAIR_DEV
    pair_ids = jnp.arange(total_pairs, dtype=jnp.int32)
    owners = (pair_ids // PAIR_DEV).astype(jnp.int32)
    living = (pair_ids % PAIR_DEV) < pair_count[owners]
    row_own = (owners * OCC_DEV + i_slot).astype(jnp.int32)
    row_far = (partner_device[:, 0] * OCC_DEV + j_slot).astype(jnp.int32)

    def visit(gamma, item):
        own_row, far_row, is_alive = item
        own_block = factors[own_row]
        far_block = factors[far_row]
        intersection = jnp.dot(own_block, far_block.T, preferred_element_type=jnp.float32)
        denominator = vir_energy[:, None] + vir_energy[None, :] - occ_energy[own_row] - occ_energy[far_row]
        amplitude = jnp.where(is_alive, intersection / denominator, jnp.zeros_like(intersection)).astype(jnp.bfloat16)
        gamma = gamma.at[own_row].add(jnp.dot(amplitude, far_block, preferred_element_type=jnp.float32))
        back_term = jnp.dot(amplitude.T, own_block, preferred_element_type=jnp.float32).astype(jnp.bfloat16)
        back_term = lax.optimization_barrier(back_term).astype(jnp.float32)
        gamma = gamma.at[far_row].add(back_term)
        return gamma, None

    start_gamma = jnp.zeros((orbitals, V, Q), jnp.float32)
    gamma = lax.scan(visit, start_gamma, (row_own, row_far, living))[0]
    rounded = gamma.astype(jnp.bfloat16).reshape(orbitals * V, Q)
    cross = jnp.dot(rounded.T, factors.reshape(orbitals * V, Q), preferred_element_type=jnp.float32)
    factor_scale = float(orbitals * V) ** -0.5
    return gamma, (cross + cross.T) * factor_scale
```

```python
import functools

import jax
import jax.numpy as jnp
from jax import lax
from jax.experimental import pallas as pl
from jax.experimental.pallas import tpu as pltpu
from jax.sharding import PartitionSpec as P


def pair_block(virtuals, own_ref, far_ref, row_ref, col_ref, weight_ref, out_ref):
    @pl.when(pl.program_id(0) == 0)
    def _():
        out_ref[...] = jnp.zeros_like(out_ref)

    far = far_ref[...]
    for k in range(own_ref.shape[0] // virtuals):
        rows = pl.ds(k * virtuals, virtuals)
        meet = lax.dot_general(
            own_ref[rows, :], far, (((1,), (1,)), ((), ())), preferred_element_type=jnp.float32
        )
        gap = row_ref[rows, :] + col_ref[...]
        amplitude = (meet / gap).astype(jnp.bfloat16) * weight_ref[k : k + 1, :].astype(jnp.bfloat16)
        out_ref[rows, :] += jnp.dot(amplitude, far, preferred_element_type=jnp.float32)


def contract(own, far, row, col, weight, virtuals, tile):
    rows, width = own.shape
    far_rows = far.shape[0]
    whole = lambda t: (0, 0)
    return pl.pallas_call(
        functools.partial(pair_block, virtuals),
        out_shape=jax.ShapeDtypeStruct((rows, width), jnp.float32),
        grid=(far_rows // tile,),
        in_specs=[
            pl.BlockSpec((rows, width), whole),
            pl.BlockSpec((tile, width), lambda t: (t, 0)),
            pl.BlockSpec((rows, 1), whole),
            pl.BlockSpec((1, tile), lambda t: (0, t)),
            pl.BlockSpec((weight.shape[0], tile), lambda t: (0, t)),
        ],
        out_specs=pl.BlockSpec((rows, width), whole),
        cost_estimate=pl.CostEstimate(
            flops=4 * rows * far_rows * width, bytes_accessed=2 * far_rows * width, transcendentals=0
        ),
        name="pair_block",
    )(own, far, row, col, weight)


def body(factors, occ_energy, vir_energy, i_slot, j_slot, partner_device, pair_count):
    held, virtuals, columns = factors.shape
    pair_slots = i_slot.shape[0]
    occ_count = lax.axis_size("occ")
    aux_count = lax.axis_size("aux")
    orbitals = occ_energy.shape[0]
    me, part = lax.axis_index("occ"), lax.axis_index("aux")
    rows = held * virtuals
    share = rows // aux_count
    parts_per_orbital = virtuals // share
    slot_of_part = part // parts_per_orbital
    first_virtual = (part % parts_per_orbital) * share

    living = jnp.arange(pair_slots, dtype=jnp.int32) < pair_count[0]
    far_index = partner_device[:, 0] * held + j_slot
    own_hot = (i_slot[:, None] == jnp.arange(held, dtype=jnp.int32)[None, :]) & living[:, None]
    far_hot = far_index[:, None] == jnp.arange(orbitals, dtype=jnp.int32)[None, :]
    counts = jnp.sum(
        (own_hot[:, :, None] & far_hot[:, None, :]).astype(jnp.int32), axis=0
    )
    sent = counts.reshape(held, occ_count, held).transpose(1, 0, 2)
    back = lax.all_to_all(sent, "occ", split_axis=0, concat_axis=0, tiled=True)
    weight = counts + back.transpose(2, 0, 1).reshape(held, orbitals)
    weight = lax.dynamic_index_in_dim(
        weight.reshape(held, occ_count, held), slot_of_part, axis=2, keepdims=False
    ).astype(jnp.float32)
    weight = jnp.broadcast_to(weight[:, :, None], (held, occ_count, share)).reshape(held, -1)

    own_energy = lax.dynamic_slice(occ_energy, (me * held,), (held,))
    row = (vir_energy[None, :] - own_energy[:, None]).reshape(rows, 1)
    far_energy = lax.dynamic_index_in_dim(
        occ_energy.reshape(occ_count, held), slot_of_part, axis=1, keepdims=False
    )
    far_virtual = lax.dynamic_slice(vir_energy, (first_virtual,), (share,))
    col = (far_virtual[None, :] - far_energy[:, None]).reshape(1, -1)

    own = lax.all_gather(factors, "aux", axis=2, tiled=True).reshape(rows, -1)
    mine = lax.dynamic_slice(own, (part * share, 0), (share, own.shape[1]))
    far = lax.all_gather(mine, "occ", axis=0, tiled=True)

    partial = contract(own, far, row, col, weight, virtuals, 4 * share)
    gamma = lax.psum_scatter(partial, "aux", scatter_dimension=1, tiled=True)
    rounded = gamma.astype(jnp.bfloat16)
    terms = lax.dot_general(
        own, rounded, (((0,), (0,)), ((), ())), preferred_element_type=jnp.float32
    )
    spread = lax.all_to_all(terms, "occ", split_axis=0, concat_axis=0, tiled=True)
    total = jnp.sum(spread.reshape(occ_count, -1, columns), axis=0)
    scale = 2.0 * float(orbitals * virtuals) ** (-0.5)
    return gamma.reshape(held, virtuals, columns), total.T * scale


def solution(mesh):
    placed = (P("occ", None, "aux"), P(), P(), P("occ"), P("occ"), P("occ", None), P("occ"))
    return jax.shard_map(
        body,
        mesh=mesh,
        in_specs=placed,
        out_specs=(P("occ", None, "aux"), P("aux", "occ")),
        check_vma=False,
    )
```

```python
import functools

import jax
import jax.numpy as jnp
import numpy as np
from jax import lax
from jax.experimental import pallas as pl
from jax.experimental.pallas import tpu as pltpu
from jax.sharding import PartitionSpec as P


GRID = {"x": 4, "z": 8, "core": 2}
STRIDE = {"x": 16, "z": 2, "core": 1}


def shift(value, axis, step):
    size, stride = GRID[axis], STRIDE[axis]
    pairs = []
    for index in range(64):
        at = index // stride % size
        pairs.append((index, index + ((at + step) % size - at) * stride))
    return lax.ppermute(value, "occ", pairs)


def turn(value, step):
    count = lax.axis_size("aux")
    return lax.ppermute(value, "aux", [(i, (i + step) % count) for i in range(count)])


class Rows:
    def __init__(self, value, places):
        self.value, self.places = value, places

    def moved(self, axis, step):
        dx, dz = (step, 0) if axis == "x" else (0, step)
        return Rows(shift(self.value, axis, step), self.places + np.array([dx, dz, 0]))

    def part(self, start, stop):
        return Rows(self.value[start:stop], self.places[start:stop])


def joined(pieces):
    return Rows(
        jnp.concatenate([p.value for p in pieces], axis=0),
        np.concatenate([p.places for p in pieces], axis=0),
    )


def gathered(mine, half):
    share = mine.shape[0]
    places = np.stack([np.zeros(share, int), np.zeros(share, int), np.arange(share)], axis=1)
    whole = Rows(mine, places)
    a, b = whole.part(0, half), whole.part(half, share)
    ap, am = a.moved("z", 1), a.moved("z", -1)
    bp, bm = b.moved("x", 1), b.moved("x", -1)
    ap2, am2 = ap.moved("z", 1), am.moved("z", -1)
    b2 = bp.moved("x", 1)
    bb = joined([b, bp, bm, b2])
    bz = {1: bb.moved("z", 1), -1: bb.moved("z", -1)}
    a1 = joined([a, ap, am, ap2, am2])
    ax1 = {1: a1.moved("x", 1), -1: a1.moved("x", -1)}
    ap3, am3 = ap2.moved("z", 1), am2.moved("z", -1)
    bz[2], bz[-2] = bz[1].moved("z", 1), bz[-1].moved("z", -1)
    ap4 = ap3.moved("z", 1)
    cut = a1.value.shape[0] // 2
    ax1[2] = ax1[1].part(0, cut).moved("x", 1)
    ax1[-2] = ax1[-1].part(cut, 2 * cut).moved("x", -1)
    a2 = joined([ap3, am3, ap4])
    ax2 = {1: a2.moved("x", 1), -1: a2.moved("x", -1)}
    bz[3], bz[-3] = bz[2].moved("z", 1), bz[-2].moved("z", -1)
    cut = bb.value.shape[0] // 2
    bz[4] = bz[3].part(0, cut).moved("z", 1)
    bz[-4] = bz[-3].part(cut, 2 * cut).moved("z", -1)
    cut = a2.value.shape[0] // 2
    ax2[2] = ax2[1].part(0, cut).moved("x", 1)
    ax2[-2] = ax2[-1].part(cut, 2 * cut).moved("x", -1)
    return [
        [bb, a1, bz[1], bz[-1], ax1[1], ax1[-1], ap3],
        [am3, ax1[2], ax1[-2], bz[2], bz[-2], bz[3], bz[-3], ax2[1], ax2[-1]],
        [ap4, bz[4], bz[-4], ax2[2], ax2[-2]],
    ], ap2.value


def pair_block(virtuals, sizes, halves, base, first, tile, *refs):
    count = len(sizes)
    own_refs, refs = refs[:halves], refs[halves:]
    row_refs, refs = refs[:halves], refs[halves:]
    col_ref, weight_ref, refs = refs[0], refs[1], refs[2:]
    piece_refs, refs = refs[:count], refs[count:]
    before_ref, refs = (None, refs) if first else (refs[0], refs[1:])
    out_ref, far, amplitude, total, piece_sem, before_sem, out_sem = refs
    fetches, start = [], 0
    for n, size in enumerate(sizes):
        copy = pltpu.make_async_copy(piece_refs[n], far.at[pl.ds(start, size)], piece_sem.at[n])
        copy.start()
        fetches.append(copy)
        start += size
    if not first:
        load = pltpu.make_async_copy(before_ref.at[pl.ds(base, halves)], total, before_sem)
        load.start()
    for copy in fetches:
        copy.wait()
    held = own_refs[0].shape[0] // virtuals
    blocks, width = total.shape[1], total.shape[3]
    stores = []
    for h in range(halves):
        own = own_refs[h][...]
        row = row_refs[h][...]

        def meet(t, _):
            span = pl.ds(pl.multiple_of(t * tile, tile), tile)
            x = lax.dot_general(
                own, far[span, :], (((1,), (1,)), ((), ())), preferred_element_type=jnp.float32
            )
            x = (x / (row + col_ref[:, span])).astype(jnp.bfloat16)
            for k in range(held):
                rows = slice(k * virtuals, (k + 1) * virtuals)
                at = h * held + k
                amplitude[rows, span] = x[rows] * weight_ref[at : at + 1, span].astype(jnp.bfloat16)
            return 0

        lax.fori_loop(0, start // tile, meet, 0)
        if h == 0 and not first:
            load.wait()

        def gain(q, _):
            span = pl.ds(pl.multiple_of(q * width, width), width)
            y = jnp.dot(amplitude[...], far[:, span], preferred_element_type=jnp.float32)
            total[h, q] = y if first else total[h, q] + y
            return 0

        lax.fori_loop(0, blocks, gain, 0)
        store = pltpu.make_async_copy(total.at[h], out_ref.at[h], out_sem.at[h])
        store.start()
        stores.append(store)
    for store in stores:
        store.wait()


def contract(owns, rows_of, pieces, col, weight, before, base, virtuals, columns, tile):
    rows, width = owns[0].shape
    sizes = tuple(p.shape[0] for p in pieces)
    far_rows = sum(sizes)
    halves = len(owns)
    first = before is None
    vmem = pl.BlockSpec(memory_space=pltpu.VMEM)
    anywhere = pl.BlockSpec(memory_space=pl.ANY)
    shape = (halves, width // columns, rows, columns)
    operands = [*owns, *rows_of, col, weight, *pieces]
    in_specs = [vmem] * (2 * halves + 2) + [anywhere] * len(pieces)
    if not first:
        operands.append(before)
        in_specs.append(anywhere)
    return pl.pallas_call(
        functools.partial(pair_block, virtuals, sizes, halves, base, first, tile),
        out_shape=jax.ShapeDtypeStruct(shape, jnp.float32),
        in_specs=in_specs,
        out_specs=anywhere,
        scratch_shapes=[
            pltpu.VMEM((far_rows, width), jnp.bfloat16),
            pltpu.VMEM((rows, far_rows), jnp.bfloat16),
            pltpu.VMEM(shape, jnp.float32),
            pltpu.SemaphoreType.DMA((len(pieces),)),
            pltpu.SemaphoreType.DMA,
            pltpu.SemaphoreType.DMA((halves,)),
        ],
        compiler_params=pltpu.CompilerParams(vmem_limit_bytes=28 << 20),
        cost_estimate=pl.CostEstimate(
            flops=4 * halves * rows * far_rows * width,
            bytes_accessed=2 * far_rows * width + 8 * halves * rows * width,
            transcendentals=0,
        ),
        name="pair_block",
    )(*operands)


def body(factors, occ_energy, vir_energy, i_slot, j_slot, partner_device, pair_count):
    held, virtuals, columns = factors.shape
    pair_slots = i_slot.shape[0]
    occ_count = lax.axis_size("occ")
    aux_count = lax.axis_size("aux")
    orbitals = occ_energy.shape[0]
    me, part = lax.axis_index("occ"), lax.axis_index("aux")
    core = me % 2
    rows = held * virtuals
    share = rows // aux_count
    parts_per_orbital = virtuals // share
    slot_of_part = part // parts_per_orbital
    first_virtual = (part % parts_per_orbital) * share

    flat = factors.reshape(rows, columns)
    mine = lax.all_to_all(flat.reshape(aux_count, share, columns), "aux", 0, 0)
    mine = mine.transpose(1, 0, 2).reshape(share, aux_count * columns)
    chunks, early = gathered(mine, share // 2)

    turned = jnp.stack([flat, turn(flat, 1), turn(flat, 2), turn(flat, -1)])
    own = jnp.concatenate(
        [
            lax.dynamic_index_in_dim(turned, (part - at) % aux_count, axis=0, keepdims=False)
            for at in range(aux_count)
        ],
        axis=1,
    )
    other = shift(own, "core", 1)

    living = jnp.arange(pair_slots, dtype=jnp.int32) < pair_count[0]
    far_index = partner_device[:, 0] * held + j_slot
    own_hot = (i_slot[:, None] == jnp.arange(held, dtype=jnp.int32)[None, :]) & living[:, None]
    far_hot = far_index[:, None] == jnp.arange(orbitals, dtype=jnp.int32)[None, :]
    counts = jnp.sum((own_hot[:, :, None] & far_hot[:, None, :]).astype(jnp.int32), axis=0)
    to_chip = counts.reshape(held, occ_count // 2, 2 * held).transpose(1, 0, 2)
    to_chip = jnp.repeat(to_chip, 2, axis=0)
    to_chip, _ = lax.optimization_barrier((to_chip, early))
    came = lax.all_to_all(to_chip, "occ", 0, 0)
    came = came.transpose(2, 0, 1).reshape(2, held, orbitals)
    weight_own = counts + lax.dynamic_index_in_dim(came, core, axis=0, keepdims=False)
    weight_other = shift(counts, "core", 1) + lax.dynamic_index_in_dim(
        came, 1 - core, axis=0, keepdims=False
    )

    energy = lambda device: lax.dynamic_slice(occ_energy, (device * held,), (held,))
    row_of = lambda device: (vir_energy[None, :] - energy(device)[:, None]).reshape(rows, 1)
    row_own, row_other = row_of(me), row_of(me + 1 - 2 * core)
    places = np.concatenate([p.places for chunk in chunks for p in chunk]).astype(np.int32)
    x, z = me // STRIDE["x"], me // STRIDE["z"] % GRID["z"]
    home = (x - jnp.asarray(places[:, 0])) % GRID["x"] * STRIDE["x"]
    home = home + (z - jnp.asarray(places[:, 1])) % GRID["z"] * STRIDE["z"] + core
    orbital = home * held + slot_of_part
    hot = orbital[None, :] == jnp.arange(orbitals, dtype=jnp.int32)[:, None]
    place_hot = jnp.asarray(places[:, 2])[None, :] == jnp.arange(share, dtype=jnp.int32)[:, None]
    far_virtual = lax.dynamic_slice(vir_energy, (first_virtual,), (share,))
    col = jnp.sum(jnp.where(place_hot, far_virtual[:, None], 0.0), axis=0)
    col = col - jnp.sum(jnp.where(hot, occ_energy[:, None], 0.0), axis=0)
    col = col[None, :]
    weights = jnp.concatenate([weight_own, weight_other]).astype(jnp.bfloat16)
    weights = jnp.dot(weights, hot.astype(jnp.bfloat16), preferred_element_type=jnp.float32)

    owns, rows_of = [own, other], [row_own, row_other]
    before, start = None, 0
    for chunk in chunks[:-1]:
        pieces = [p.value for p in chunk]
        span = slice(start, start + sum(p.shape[0] for p in pieces))
        start = span.stop
        before = contract(
            owns, rows_of, pieces, col[:, span], weights[:, span], before, 0, virtuals, columns, 256
        )
    pieces = [p.value for p in chunks[-1]]
    last = [
        contract(
            owns[h : h + 1],
            rows_of[h : h + 1],
            pieces,
            col[:, start:],
            weights[h * held : (h + 1) * held, start:],
            before,
            h,
            virtuals,
            columns,
            256,
        )[0]
        for h in (0, 1)
    ]
    partial = last[0] + shift(last[1], "core", 1)
    sliced = lax.all_to_all(partial, "aux", 0, 0)
    gamma = jnp.sum(sliced, axis=0)
    rounded = gamma.astype(jnp.bfloat16)
    terms = lax.dot_general(
        own, rounded, (((0,), (0,)), ((), ())), preferred_element_type=jnp.float32
    )
    terms = terms.reshape(occ_count // 2, 2, -1, columns)
    kept = lax.dynamic_index_in_dim(terms, core, axis=1, keepdims=False)
    given = lax.dynamic_index_in_dim(terms, 1 - core, axis=1, keepdims=False)
    kept = kept + shift(given, "core", 1)
    groups = [[2 * i + c for i in range(occ_count // 2)] for c in range(2)]
    spread = lax.all_to_all(kept, "occ", 0, 0, axis_index_groups=groups)
    total = jnp.sum(spread, axis=0)
    scale = 2.0 * float(orbitals * virtuals) ** (-0.5)
    return gamma.reshape(held, virtuals, columns), total.T * scale


def solution(mesh):
    placed = (P("occ", None, "aux"), P(), P(), P("occ"), P("occ"), P("occ", None), P("occ"))
    return jax.shard_map(
        body,
        mesh=mesh,
        in_specs=placed,
        out_specs=(P("occ", None, "aux"), P("aux", "occ")),
        check_vma=False,
    )
```

```python
import functools

import jax
import jax.numpy as jnp
import numpy as np
from jax import lax
from jax.experimental import pallas as pl
from jax.experimental.pallas import tpu as pltpu
from jax.sharding import PartitionSpec as P


GRID = {"x": 4, "z": 8, "core": 2}
STRIDE = {"x": 16, "z": 2, "core": 1}


def shift(value, axis, step):
    size, stride = GRID[axis], STRIDE[axis]
    pairs = []
    for index in range(64):
        at = index // stride % size
        pairs.append((index, index + ((at + step) % size - at) * stride))
    return lax.ppermute(value, "occ", pairs)


def turn(value, step):
    count = lax.axis_size("aux")
    return lax.ppermute(value, "aux", [(i, (i + step) % count) for i in range(count)])


class Rows:
    def __init__(self, value, places):
        self.value, self.places = value, places

    def moved(self, axis, step):
        dx, dz = (step, 0) if axis == "x" else (0, step)
        return Rows(shift(self.value, axis, step), self.places + np.array([dx, dz, 0]))

    def part(self, start, stop):
        return Rows(self.value[start:stop], self.places[start:stop])


def joined(pieces):
    return Rows(
        jnp.concatenate([p.value for p in pieces], axis=0),
        np.concatenate([p.places for p in pieces], axis=0),
    )


class Gather:
    def __init__(self, share, half):
        self.share, self.half = share, half

    def first(self, mine):
        share, half = self.share, self.half
        places = np.stack([np.zeros(share, int), np.zeros(share, int), np.arange(share)], axis=1)
        whole = Rows(mine, places)
        a, b = whole.part(0, half), whole.part(half, share)
        ap, am = a.moved("z", 1), a.moved("z", -1)
        bp, bm = b.moved("x", 1), b.moved("x", -1)
        ap2, am2 = ap.moved("z", 1), am.moved("z", -1)
        b2 = bp.moved("x", 1)
        self.later = ap2.value
        bb = joined([b, bp, bm, b2])
        a1 = joined([a, ap, am, ap2, am2])
        bz1, bzm1 = bb.moved("z", 1), bb.moved("z", -1)
        ap3, am3 = ap2.moved("z", 1), am2.moved("z", -1)
        ax1, axm1 = a1.moved("x", 1), a1.moved("x", -1)
        self.cuts = [2 * half, 3 * half]
        cut = self.cuts[1]
        self.ap4 = ap3.moved("z", 1)
        self.latest = self.ap4.value
        self.bz2, self.bzm2 = bz1.moved("z", 1), bzm1.moved("z", -1)
        ax2, axm2 = ax1.part(0, cut).moved("x", 1), axm1.part(cut, 5 * half).moved("x", -1)
        self.a2 = joined([ap3, am3, self.ap4])
        self.second_chunk = [am3, ax2, axm2, self.bz2, self.bzm2]
        return [bb, a1, bz1, bzm1, ax1, axm1, ap3]

    def second(self):
        bz2, bzm2, a2 = self.bz2, self.bzm2, self.a2
        self.bz3, self.bzm3 = bz2.moved("z", 1), bzm2.moved("z", -1)
        self.cx1, self.cxm1 = a2.moved("x", 1), a2.moved("x", -1)
        self.third_chunk = [self.bz3, self.bzm3, self.cx1, self.cxm1]
        return self.second_chunk

    def third(self):
        bz3, bzm3, cx1, cxm1 = self.third_chunk
        cut = self.cuts[0]
        bz4, bzm4 = bz3.part(0, cut).moved("z", 1), bzm3.part(cut, 2 * cut).moved("z", -1)
        cx2, cxm2 = cx1.part(0, cut).moved("x", 1), cxm1.part(cut, cxm1.value.shape[0]).moved("x", -1)
        self.last_chunk = [self.ap4, bz4, bzm4, cx2, cxm2]
        return self.third_chunk


def pair_block(virtuals, sizes, unit, first, *refs):
    count, units = len(sizes), sum(sizes) // unit
    here_ref, code_ref, sent_ref, came_ref, energy_ref, vir_ref, *refs = refs
    own_refs, row_refs, refs = refs[:2], refs[2:4], refs[4:]
    piece_refs, refs = refs[:count], refs[count:]
    before_refs, refs = ([], refs) if first else (refs[:2], refs[2:])
    out_refs, refs = refs[:2], refs[2:]
    far, near, total, chosen, times, piece_sem, before_sem, out_sem = refs
    fetches, start = [], 0
    for n, size in enumerate(sizes):
        copy = pltpu.make_async_copy(piece_refs[n], far.at[pl.ds(start, size)], piece_sem.at[n])
        copy.start()
        fetches.append(copy)
        start += size
    for h, before_ref in enumerate(before_refs):
        copy = pltpu.make_async_copy(before_ref, total.at[h], before_sem.at[h])
        copy.start()
        fetches.append(copy)
    if first:
        total[...] = jnp.zeros_like(total)
    for copy in fetches:
        copy.wait()
    held = own_refs[0].shape[0] // virtuals
    blocks, width = total.shape[1], total.shape[3]
    part, slot = here_ref[0], here_ref[1]
    group = near.shape[0] // unit
    lane = lax.broadcasted_iota(jnp.int32, (1, near.shape[0]), 1) // unit
    stores = []
    for h in (1, 0):
        for k in range(held):
            rows = slice(k * virtuals, (k + 1) * virtuals)
            at = h * held + k

            def scan(p, n):
                home = code_ref[p] >> 1
                w = sent_ref[at, home] + came_ref[home, at]
                chosen[n] = p
                times[n] = w
                return n + jnp.where(w > 0, 1, 0)

            live = lax.fori_loop(0, units, scan, jnp.int32(0), unroll=2)
            for j in range(group):
                chosen[live + j] = 0
                times[live + j] = 0

            def tile(t, _):
                col = jnp.zeros(lane.shape, jnp.float32)
                weight = jnp.zeros(lane.shape, jnp.float32)
                for j in range(group):
                    p = chosen[t * group + j]
                    code = code_ref[p]
                    near[j * unit : (j + 1) * unit, :] = far[pl.ds(pl.multiple_of(p * unit, unit), unit), :]
                    energy = energy_ref[(code >> 1) * held + slot]
                    upper = (code & 1).astype(jnp.float32)
                    value = vir_ref[0:1, :] * (1.0 - upper) + vir_ref[1:2, :] * upper - energy
                    col = jnp.where(lane == j, value, col)
                    weight = jnp.where(lane == j, times[t * group + j].astype(jnp.float32), weight)
                x = lax.dot_general(
                    own_refs[h][rows, :],
                    near[...],
                    (((1,), (1,)), ((), ())),
                    preferred_element_type=jnp.float32,
                )
                x = (x / (row_refs[h][rows, :] + col)).astype(jnp.bfloat16) * weight.astype(jnp.bfloat16)
                for q in range(blocks):
                    y = jnp.dot(
                        x, near[:, q * width : (q + 1) * width], preferred_element_type=jnp.float32
                    )
                    place = lax.rem(q + blocks - part, blocks)
                    total[h, place, rows, :] += y
                return 0

            lax.fori_loop(0, (live + group - 1) // group, tile, 0)
        store = pltpu.make_async_copy(total.at[h], out_refs[h], out_sem.at[h])
        store.start()
        stores.append(store)
    for store in stores:
        store.wait()


def contract(here, codes, sent, came, energy, vir, owns, rows_of, pieces, before, virtuals, columns):
    rows, width = owns[0].shape
    unit = vir.shape[1] // 4
    sizes = tuple(p.value.shape[0] for p in pieces)
    far_rows = sum(sizes)
    first = before is None
    smem = pl.BlockSpec(memory_space=pltpu.SMEM)
    vmem = pl.BlockSpec(memory_space=pltpu.VMEM)
    anywhere = pl.BlockSpec(memory_space=pl.ANY)
    shape = (width // columns, rows, columns)
    operands = [here, codes(pieces, unit), sent, came, energy, vir, *owns, *rows_of]
    operands += [p.value for p in pieces] + ([] if first else list(before))
    in_specs = [smem] * 5 + [vmem] * 5 + [anywhere] * (len(operands) - 10)
    return pl.pallas_call(
        functools.partial(pair_block, virtuals, sizes, unit, first),
        out_shape=[jax.ShapeDtypeStruct(shape, jnp.float32)] * 2,
        in_specs=in_specs,
        out_specs=[anywhere] * 2,
        scratch_shapes=[
            pltpu.VMEM((far_rows, width), jnp.bfloat16),
            pltpu.VMEM((4 * unit, width), jnp.bfloat16),
            pltpu.VMEM((2,) + shape, jnp.float32),
            pltpu.SMEM((far_rows // unit + 4,), jnp.int32),
            pltpu.SMEM((far_rows // unit + 4,), jnp.int32),
            pltpu.SemaphoreType.DMA((len(pieces),)),
            pltpu.SemaphoreType.DMA((2,)),
            pltpu.SemaphoreType.DMA((2,)),
        ],
        compiler_params=pltpu.CompilerParams(vmem_limit_bytes=28 << 20),
        cost_estimate=pl.CostEstimate(
            flops=2 * rows * far_rows * width,
            bytes_accessed=2 * far_rows * width + 16 * rows * width,
            transcendentals=0,
        ),
        name="pair_block",
    )(*operands)


def body(factors, occ_energy, vir_energy, i_slot, j_slot, partner_device, pair_count):
    held, virtuals, columns = factors.shape
    pair_slots = i_slot.shape[0]
    occ_count = lax.axis_size("occ")
    aux_count = lax.axis_size("aux")
    orbitals = occ_energy.shape[0]
    me, part = lax.axis_index("occ"), lax.axis_index("aux")
    core = me % 2
    rows = held * virtuals
    share = rows // aux_count
    parts_per_orbital = virtuals // share
    slot_of_part = part // parts_per_orbital
    first_virtual = (part % parts_per_orbital) * share

    flat = factors.reshape(rows, columns)
    mine = lax.all_to_all(flat.reshape(aux_count, share, columns), "aux", 0, 0)
    mine = mine.transpose(1, 0, 2).reshape(share, aux_count * columns)
    gather = Gather(share, share // 2)
    pieces = gather.first(mine)

    late, _ = lax.optimization_barrier((flat, gather.later))
    turned = jnp.stack([flat, turn(late, 1), turn(late, 2), turn(late, -1)])
    own = jnp.concatenate(
        [
            lax.dynamic_index_in_dim(turned, (part - at) % aux_count, axis=0, keepdims=False)
            for at in range(aux_count)
        ],
        axis=1,
    )
    owns = [own, shift(own, "core", 1)]

    living = jnp.arange(pair_slots, dtype=jnp.int32) < pair_count[0]
    target = partner_device[:, 0]
    own_hot = (i_slot[:, None] == jnp.arange(held, dtype=jnp.int32)[None, :]) & living[:, None]
    far_hot = target[:, None] == jnp.arange(occ_count, dtype=jnp.int32)[None, :]
    far_hot = far_hot & (j_slot == slot_of_part)[:, None]
    counts = jnp.sum((own_hot[:, :, None] & far_hot[:, None, :]).astype(jnp.int32), axis=0)
    sent = jnp.concatenate([counts, shift(counts, "core", 1), jnp.zeros((4, occ_count), jnp.int32)])
    column = np.arange(8)[None, :]
    wanted = np.where(column < 2 * held, np.arange(occ_count)[:, None] ^ (column // held), -1)
    wanted_slot = np.broadcast_to(column % held, wanted.shape)
    match = (target[:, None, None] == jnp.asarray(wanted, jnp.int32)[None]) & (
        j_slot[:, None, None] == jnp.asarray(wanted_slot, jnp.int32)[None]
    )
    match = match & ((i_slot == slot_of_part) & living)[:, None, None]
    to_chip = jnp.sum(match.astype(jnp.int32), axis=0)
    to_chip, _ = lax.optimization_barrier((to_chip, gather.latest))
    came = lax.all_to_all(to_chip, "occ", 0, 0, tiled=True)

    energy = lambda device: lax.dynamic_slice(occ_energy, (device * held,), (held,))
    row_of = lambda device: (vir_energy[None, :] - energy(device)[:, None]).reshape(rows, 1)
    rows_of = [row_of(me), row_of(me + 1 - 2 * core)]
    x, z = me // STRIDE["x"], me // STRIDE["z"] % GRID["z"]
    far_virtual = lax.dynamic_slice(vir_energy, (first_virtual,), (share,)).reshape(2, -1)
    far_virtual = jnp.tile(far_virtual, (1, 4))
    here = jnp.stack([part, slot_of_part]).astype(jnp.int32)

    def codes(pieces, unit):
        places = np.concatenate([p.places for p in pieces])[::unit].astype(np.int32)
        home = (x - jnp.asarray(places[:, 0])) % GRID["x"] * STRIDE["x"]
        home = home + (z - jnp.asarray(places[:, 1])) % GRID["z"] * STRIDE["z"] + core
        return home * 2 + jnp.asarray(places[:, 2] // unit)

    run = lambda pieces, before: contract(
        here, codes, sent, came, occ_energy, far_virtual, owns, rows_of, pieces, before, virtuals, columns
    )
    pieces = pieces + gather.second()
    total = run(pieces, None)
    total = run(gather.third(), total)
    total = run(gather.last_chunk, total)
    partial = total[0] + shift(total[1], "core", 1)
    up, down = partial[:, :virtuals], partial[:, virtuals:]
    came_up, came_down = turn(up[2], 1), turn(down[2], -1)
    up3, down1, came_up, came_down = lax.optimization_barrier((up[3], down[1], came_up, came_down))
    up_sum = up[0] + turn(up[1] + came_up, 1) + turn(up3, -1)
    down_sum = down[0] + turn(down1, 1) + turn(down[3] + came_down, -1)
    gamma = jnp.concatenate([up_sum, down_sum])
    rounded = gamma.astype(jnp.bfloat16)
    terms = lax.dot_general(
        own, rounded, (((0,), (0,)), ((), ())), preferred_element_type=jnp.float32
    )
    terms = terms.reshape(occ_count // 2, 2, -1, columns)
    kept = lax.dynamic_index_in_dim(terms, core, axis=1, keepdims=False)
    given = lax.dynamic_index_in_dim(terms, 1 - core, axis=1, keepdims=False)
    kept = kept + shift(given, "core", 1)
    groups = [[2 * i + c for i in range(occ_count // 2)] for c in range(2)]
    spread = lax.all_to_all(kept, "occ", 0, 0, axis_index_groups=groups)
    total = jnp.sum(spread, axis=0)
    scale = 2.0 * float(orbitals * virtuals) ** (-0.5)
    return gamma.reshape(held, virtuals, columns), total.T * scale


def solution(mesh):
    placed = (P("occ", None, "aux"), P(), P(), P("occ"), P("occ"), P("occ", None), P("occ"))
    return jax.shard_map(
        body,
        mesh=mesh,
        in_specs=placed,
        out_specs=(P("occ", None, "aux"), P("aux", "occ")),
        check_vma=False,
    )
```

```python
import functools

import jax
import jax.numpy as jnp
import numpy as np
from jax import lax
from jax.experimental import pallas as pl
from jax.experimental.pallas import tpu as pltpu
from jax.sharding import PartitionSpec as P


GRID = {"x": 4, "z": 8, "core": 2}
STRIDE = {"x": 16, "z": 2, "core": 1}


def shift(value, axis, step):
    size, stride = GRID[axis], STRIDE[axis]
    pairs = []
    for index in range(64):
        at = index // stride % size
        pairs.append((index, index + ((at + step) % size - at) * stride))
    return lax.ppermute(value, "occ", pairs)


class Rows:
    def __init__(self, value, places):
        self.value, self.places = value, places

    def moved(self, axis, step):
        dx, dz = (step, 0) if axis == "x" else (0, step)
        return Rows(shift(self.value, axis, step), self.places + np.array([dx, dz, 0]))

    def part(self, start, stop):
        return Rows(self.value[start:stop], self.places[start:stop])


def joined(pieces):
    return Rows(
        jnp.concatenate([p.value for p in pieces], axis=0),
        np.concatenate([p.places for p in pieces], axis=0),
    )


def gathered(mine, half):
    share = mine.shape[0]
    places = np.stack([np.zeros(share, int), np.zeros(share, int), np.arange(share)], axis=1)
    whole = Rows(mine, places)
    a, b = whole.part(0, half), whole.part(half, share)
    ap, am = a.moved("z", 1), a.moved("z", -1)
    bp, bm = b.moved("x", 1), b.moved("x", -1)
    ap2, am2 = ap.moved("z", 1), am.moved("z", -1)
    b2 = bp.moved("x", 1)
    bb = joined([b, bp, bm, b2])
    a1 = joined([a, ap, am, ap2, am2])
    bz1, bzm1 = bb.moved("z", 1), bb.moved("z", -1)
    ap3, am3 = ap2.moved("z", 1), am2.moved("z", -1)
    ax1, axm1 = a1.moved("x", 1), a1.moved("x", -1)
    am4 = am3.moved("z", -1)
    bz2, bzm2 = bz1.moved("z", 1), bzm1.moved("z", -1)
    ax2 = ax1.moved("x", 1)
    a2 = joined([ap3, am3, am4])
    bz3, bzm3 = bz2.moved("z", 1), bzm2.moved("z", -1)
    cx1, cxm1 = a2.moved("x", 1), a2.moved("x", -1)
    bz4 = bz3.moved("z", 1)
    cxm2 = cxm1.moved("x", -1)
    return [
        [bb, a1, bz1, bzm1, ax1, axm1, ap3, am3, am4, ax2, bz2, bzm2],
        [bz3, bzm3, cx1, cxm1],
        [bz4, cxm2],
    ], bz1.value


def pair_block(virtuals, sizes, unit, first, *refs):
    count, units = len(sizes), sum(sizes) // unit
    here_ref, code_ref, sent_ref, came_ref, energy_ref, vir_ref, *refs = refs
    own_refs, row_refs, refs = refs[:2], refs[2:4], refs[4:]
    piece_refs, refs = refs[:count], refs[count:]
    before_refs, refs = ([], refs) if first else (refs[:2], refs[2:])
    out_refs, refs = refs[:2], refs[2:]
    far, near, total, chosen, times, piece_sem, before_sem, out_sem = refs
    fetches, start = [], 0
    for n, size in enumerate(sizes):
        copy = pltpu.make_async_copy(piece_refs[n], far.at[pl.ds(start, size)], piece_sem.at[n])
        copy.start()
        fetches.append(copy)
        start += size
    for h, before_ref in enumerate(before_refs):
        copy = pltpu.make_async_copy(before_ref, total.at[h], before_sem.at[h])
        copy.start()
        fetches.append(copy)
    if first:
        total[...] = jnp.zeros_like(total)
    for copy in fetches:
        copy.wait()
    held = own_refs[0].shape[0] // virtuals
    blocks, width = total.shape[1], total.shape[3]
    part = here_ref[0]
    slot, window = part // 2, part % 2 * 2
    group = near.shape[0] // unit
    lane = lax.broadcasted_iota(jnp.int32, (1, near.shape[0]), 1) // unit
    stores = []
    for h in (1, 0):
        for k in range(held):
            rows = slice(k * virtuals, (k + 1) * virtuals)
            at = h * held + k

            def scan(p, n):
                home = code_ref[p] >> 1
                w = sent_ref[at, home] + came_ref[home, at]
                chosen[n] = p
                times[n] = w
                return n + jnp.where(w > 0, 1, 0)

            live = lax.fori_loop(0, units, scan, jnp.int32(0), unroll=2)
            for j in range(group):
                chosen[live + j] = 0
                times[live + j] = 0

            def tile(t, _):
                col = jnp.zeros(lane.shape, jnp.float32)
                weight = jnp.zeros(lane.shape, jnp.float32)
                for j in range(group):
                    p = chosen[t * group + j]
                    code = code_ref[p]
                    near[j * unit : (j + 1) * unit, :] = far[pl.ds(pl.multiple_of(p * unit, unit), unit), :]
                    energy = energy_ref[(code >> 1) * held + slot]
                    value = vir_ref[pl.ds(window + (code & 1), 1), :] - energy
                    col = jnp.where(lane == j, value, col)
                    weight = jnp.where(lane == j, times[t * group + j].astype(jnp.float32), weight)
                x = lax.dot_general(
                    own_refs[h][rows, :],
                    near[...],
                    (((1,), (1,)), ((), ())),
                    preferred_element_type=jnp.float32,
                )
                x = (x / (row_refs[h][rows, :] + col)).astype(jnp.bfloat16) * weight.astype(jnp.bfloat16)
                for q in range(blocks):
                    y = jnp.dot(
                        x, near[:, q * width : (q + 1) * width], preferred_element_type=jnp.float32
                    )
                    total[h, q, rows, :] += y
                return 0

            lax.fori_loop(0, (live + group - 1) // group, tile, 0)
        store = pltpu.make_async_copy(total.at[h], out_refs[h], out_sem.at[h])
        store.start()
        stores.append(store)
    for store in stores:
        store.wait()


def contract(here, codes, sent, came, energy, vir, owns, rows_of, pieces, before, virtuals, columns):
    rows, width = owns[0].shape
    unit = vir.shape[1] // 4
    sizes = tuple(p.value.shape[0] for p in pieces)
    far_rows = sum(sizes)
    first = before is None
    smem = pl.BlockSpec(memory_space=pltpu.SMEM)
    vmem = pl.BlockSpec(memory_space=pltpu.VMEM)
    hbm = pl.BlockSpec(memory_space=pltpu.HBM)
    shape = (width // columns, rows, columns)
    operands = [here, codes(pieces, unit), sent, came, energy, vir, *owns, *rows_of]
    operands += [p.value for p in pieces] + ([] if first else list(before))
    in_specs = [smem] * 5 + [vmem] * 5 + [hbm] * (len(operands) - 10)
    return pl.pallas_call(
        functools.partial(pair_block, virtuals, sizes, unit, first),
        out_shape=[jax.ShapeDtypeStruct(shape, jnp.float32)] * 2,
        in_specs=in_specs,
        out_specs=[hbm] * 2,
        scratch_shapes=[
            pltpu.VMEM((far_rows, width), jnp.bfloat16),
            pltpu.VMEM((4 * unit, width), jnp.bfloat16),
            pltpu.VMEM((2,) + shape, jnp.float32),
            pltpu.SMEM((far_rows // unit + 4,), jnp.int32),
            pltpu.SMEM((far_rows // unit + 4,), jnp.int32),
            pltpu.SemaphoreType.DMA((len(pieces),)),
            pltpu.SemaphoreType.DMA((2,)),
            pltpu.SemaphoreType.DMA((2,)),
        ],
        compiler_params=pltpu.CompilerParams(vmem_limit_bytes=28 << 20),
        cost_estimate=pl.CostEstimate(
            flops=2 * rows * far_rows * width,
            bytes_accessed=2 * far_rows * width + 16 * rows * width,
            transcendentals=0,
        ),
        name="pair_block",
    )(*operands)


def body(factors, occ_energy, vir_energy, i_slot, j_slot, partner_device, pair_count):
    held, virtuals, columns = factors.shape
    pair_slots = i_slot.shape[0]
    occ_count = lax.axis_size("occ")
    aux_count = lax.axis_size("aux")
    orbitals = occ_energy.shape[0]
    me, part = lax.axis_index("occ"), lax.axis_index("aux")
    core = me % 2
    rows = held * virtuals
    share = rows // aux_count
    parts_per_orbital = virtuals // share
    slot_of_part = part // parts_per_orbital

    flat = factors.reshape(rows, columns)
    turned = lax.all_to_all(jnp.broadcast_to(flat, (aux_count, rows, columns)), "aux", 0, 0)
    mine = lax.dynamic_slice(turned, (0, part * share, 0), (aux_count, share, columns))
    mine = mine.transpose(1, 0, 2).reshape(share, -1)
    chunks, late = gathered(mine, share // 2)
    own = turned.transpose(1, 0, 2).reshape(rows, -1)
    owns = [own, shift(own, "core", 1)]

    living = jnp.arange(pair_slots, dtype=jnp.int32) < pair_count[0]
    target = partner_device[:, 0]
    own_hot = (i_slot[:, None] == jnp.arange(held, dtype=jnp.int32)[None, :]) & living[:, None]
    far_hot = target[:, None] == jnp.arange(occ_count, dtype=jnp.int32)[None, :]
    far_hot = far_hot & (j_slot == slot_of_part)[:, None]
    counts = jnp.sum((own_hot[:, :, None] & far_hot[:, None, :]).astype(jnp.int32), axis=0)
    sent = jnp.concatenate([counts, shift(counts, "core", 1), jnp.zeros((4, occ_count), jnp.int32)])
    column = np.arange(8)[None, :]
    wanted = np.where(column < 2 * held, np.arange(occ_count)[:, None] ^ (column // held), -1)
    wanted_slot = np.broadcast_to(column % held, wanted.shape)
    match = (target[:, None, None] == jnp.asarray(wanted, jnp.int32)[None]) & (
        j_slot[:, None, None] == jnp.asarray(wanted_slot, jnp.int32)[None]
    )
    match = match & ((i_slot == slot_of_part) & living)[:, None, None]
    to_chip = jnp.sum(match.astype(jnp.int32), axis=0)
    to_chip, _ = lax.optimization_barrier((to_chip, late))
    came = lax.all_to_all(to_chip, "occ", 0, 0, tiled=True)

    energy = lambda device: lax.dynamic_slice(occ_energy, (device * held,), (held,))
    row_of = lambda device: (vir_energy[None, :] - energy(device)[:, None]).reshape(rows, 1)
    rows_of = [row_of(me), row_of(me + 1 - 2 * core)]
    x, z = me // STRIDE["x"], me // STRIDE["z"] % GRID["z"]
    spot = np.arange(virtuals)[None, :] % 64 + np.arange(virtuals // 64)[:, None] * 64
    spot = jnp.asarray(spot, jnp.int32)[None] == jnp.arange(virtuals, dtype=jnp.int32)[:, None, None]
    windows = jnp.sum(jnp.where(spot, vir_energy[:, None, None], 0.0), axis=0)
    here = part.astype(jnp.int32).reshape(1)

    def codes(pieces, unit):
        places = np.concatenate([p.places for p in pieces])[::unit].astype(np.int32)
        home = (x - jnp.asarray(places[:, 0])) % GRID["x"] * STRIDE["x"]
        home = home + (z - jnp.asarray(places[:, 1])) % GRID["z"] * STRIDE["z"] + core
        return home * 2 + jnp.asarray(places[:, 2] // unit)

    run = lambda pieces, before: contract(
        here, codes, sent, came, occ_energy, windows, owns, rows_of, pieces, before, virtuals, columns
    )
    total = None
    for pieces in chunks:
        total = run(pieces, total)
    partial = total[0] + shift(total[1], "core", 1)
    gamma = jnp.sum(lax.all_to_all(partial, "aux", 0, 0), axis=0)
    rounded = gamma.astype(jnp.bfloat16)
    terms = lax.dot_general(
        own, rounded, (((0,), (0,)), ((), ())), preferred_element_type=jnp.float32
    )
    terms = terms.reshape(occ_count // 2, 2, -1, columns)
    kept = lax.dynamic_index_in_dim(terms, core, axis=1, keepdims=False)
    given = lax.dynamic_index_in_dim(terms, 1 - core, axis=1, keepdims=False)
    kept = kept + shift(given, "core", 1)
    groups = [[2 * i + c for i in range(occ_count // 2)] for c in range(2)]
    spread = lax.all_to_all(kept, "occ", 0, 0, axis_index_groups=groups)
    total = jnp.sum(spread, axis=0)
    scale = 2.0 * float(orbitals * virtuals) ** (-0.5)
    return gamma.reshape(held, virtuals, columns), total.T * scale


def solution(mesh):
    placed = (P("occ", None, "aux"), P(), P(), P("occ"), P("occ"), P("occ", None), P("occ"))
    return jax.shard_map(
        body,
        mesh=mesh,
        in_specs=placed,
        out_specs=(P("occ", None, "aux"), P("aux", "occ")),
        check_vma=False,
    )
```

```python
import functools

import jax
import jax.numpy as jnp
import numpy as np
from jax import lax
from jax.experimental import pallas as pl
from jax.experimental.pallas import tpu as pltpu
from jax.sharding import PartitionSpec as P


GRID = {"x": 4, "z": 8, "core": 2}
STRIDE = {"x": 16, "z": 2, "core": 1}


def shift(value, axis, step):
    size, stride = GRID[axis], STRIDE[axis]
    pairs = []
    for index in range(64):
        at = index // stride % size
        pairs.append((index, index + ((at + step) % size - at) * stride))
    return lax.ppermute(value, "occ", pairs)


class Rows:
    def __init__(self, value, places):
        self.value, self.places = value, places

    def moved(self, axis, step):
        dx, dz = (step, 0) if axis == "x" else (0, step)
        return Rows(shift(self.value, axis, step), self.places + np.array([dx, dz, 0]))

    def part(self, start, stop):
        return Rows(self.value[start:stop], self.places[start:stop])


def joined(pieces):
    return Rows(
        jnp.concatenate([p.value for p in pieces], axis=0),
        np.concatenate([p.places for p in pieces], axis=0),
    )


def gathered(mine, half):
    share = mine.shape[0]
    places = np.stack([np.zeros(share, int), np.zeros(share, int), np.arange(share)], axis=1)
    whole = Rows(mine, places)
    a, b = whole.part(0, half), whole.part(half, share)
    ap, am = a.moved("z", 1), a.moved("z", -1)
    bp, bm = b.moved("x", 1), b.moved("x", -1)
    ap2, am2 = ap.moved("z", 1), am.moved("z", -1)
    b2 = bp.moved("x", 1)
    bb = joined([b, bp, bm, b2])
    a1 = joined([a, ap, am, ap2, am2])
    bz1, bzm1 = bb.moved("z", 1), bb.moved("z", -1)
    ap3, am3 = ap2.moved("z", 1), am2.moved("z", -1)
    ax1, axm1 = a1.moved("x", 1), a1.moved("x", -1)
    am4 = am3.moved("z", -1)
    bz2, bzm2 = bz1.moved("z", 1), bzm1.moved("z", -1)
    ax2 = ax1.moved("x", 1)
    a2 = joined([ap3, am3, am4])
    bz3, bzm3 = bz2.moved("z", 1), bzm2.moved("z", -1)
    cx1, cxm1 = a2.moved("x", 1), a2.moved("x", -1)
    bz4 = bz3.moved("z", 1)
    cxm2 = cxm1.moved("x", -1)
    return [
        [bb, a1, bz1, bzm1, ax1, axm1, ap3],
        [am3, ax2, bz2, bzm2, bz3, bzm3, cx1, cxm1],
        [am4, bz4, cxm2],
    ], ap2.value


def pair_block(virtuals, sizes, halves, base, first, tile, *refs):
    count = len(sizes)
    own_refs, refs = refs[:halves], refs[halves:]
    row_refs, refs = refs[:halves], refs[halves:]
    (col_ref, home_ref, sent_ref, came_ref), refs = refs[:4], refs[4:]
    piece_refs, refs = refs[:count], refs[count:]
    before_ref, refs = (None, refs) if first else (refs[0], refs[1:])
    out_ref, far, amplitude, weight, total, piece_sem, before_sem, out_sem = refs
    fetches, start = [], 0
    for n, size in enumerate(sizes):
        copy = pltpu.make_async_copy(piece_refs[n], far.at[pl.ds(start, size)], piece_sem.at[n])
        copy.start()
        fetches.append(copy)
        start += size
    if not first:
        load = pltpu.make_async_copy(before_ref.at[pl.ds(base, halves)], total, before_sem)
        load.start()
    devices = came_ref.shape[0]
    hot = lax.broadcasted_iota(jnp.int32, (devices, start), 0) == home_ref[...]
    hot = jnp.where(hot, 1.0, 0.0).astype(jnp.bfloat16)
    narrow = lambda ref: ref[...].astype(jnp.float32).astype(jnp.bfloat16)
    weight[...] = jnp.dot(narrow(sent_ref), hot, preferred_element_type=jnp.float32) + lax.dot_general(
        narrow(came_ref), hot, (((0,), (0,)), ((), ())), preferred_element_type=jnp.float32
    )
    for copy in fetches:
        copy.wait()
    held = own_refs[0].shape[0] // virtuals
    blocks, width = total.shape[1], total.shape[3]
    stores = []
    for h in range(halves):

        def meet(span):
            x = lax.dot_general(
                own_refs[h][...],
                far[span, :],
                (((1,), (1,)), ((), ())),
                preferred_element_type=jnp.float32,
            )
            x = (x / (row_refs[h][...] + col_ref[:, span])).astype(jnp.bfloat16)
            for k in range(held):
                rows = slice(k * virtuals, (k + 1) * virtuals)
                at = (base + h) * held + k
                amplitude[rows, span] = x[rows] * weight[at : at + 1, span].astype(jnp.bfloat16)

        def step(t, _):
            meet(pl.ds(pl.multiple_of(t * tile, tile), tile))
            return 0

        lax.fori_loop(0, start // tile, step, 0)
        if start % tile:
            meet(pl.ds(start // tile * tile, start % tile))
        if h == 0 and not first:
            load.wait()

        def gain(q, _):
            span = pl.ds(pl.multiple_of(q * width, width), width)
            y = jnp.dot(amplitude[...], far[:, span], preferred_element_type=jnp.float32)
            total[h, q] = y if first else total[h, q] + y
            return 0

        lax.fori_loop(0, blocks, gain, 0)
        store = pltpu.make_async_copy(total.at[h], out_ref.at[h], out_sem.at[h])
        store.start()
        stores.append(store)
    for store in stores:
        store.wait()


def contract(owns, rows_of, pieces, tables, sent, came, before, base, virtuals, columns):
    rows, width = owns[0].shape
    sizes = tuple(p.value.shape[0] for p in pieces)
    far_rows = sum(sizes)
    halves = len(owns)
    first = before is None
    vmem = pl.BlockSpec(memory_space=pltpu.VMEM)
    anywhere = pl.BlockSpec(memory_space=pl.ANY)
    shape = (halves, width // columns, rows, columns)
    col, home = tables(pieces)
    operands = [*owns, *rows_of, col, home, sent, came, *[p.value for p in pieces]]
    in_specs = [vmem] * (2 * halves + 4) + [anywhere] * len(pieces)
    if not first:
        operands.append(before)
        in_specs.append(anywhere)
    return pl.pallas_call(
        functools.partial(pair_block, virtuals, sizes, halves, base, first, 256),
        out_shape=jax.ShapeDtypeStruct(shape, jnp.float32),
        in_specs=in_specs,
        out_specs=anywhere,
        scratch_shapes=[
            pltpu.VMEM((far_rows, width), jnp.bfloat16),
            pltpu.VMEM((rows, far_rows), jnp.bfloat16),
            pltpu.VMEM((sent.shape[0], far_rows), jnp.float32),
            pltpu.VMEM(shape, jnp.float32),
            pltpu.SemaphoreType.DMA((len(pieces),)),
            pltpu.SemaphoreType.DMA,
            pltpu.SemaphoreType.DMA((halves,)),
        ],
        compiler_params=pltpu.CompilerParams(vmem_limit_bytes=28 << 20),
        cost_estimate=pl.CostEstimate(
            flops=4 * halves * rows * far_rows * width,
            bytes_accessed=2 * far_rows * width + 8 * halves * rows * width,
            transcendentals=0,
        ),
        name="pair_block",
    )(*operands)


def body(factors, occ_energy, vir_energy, i_slot, j_slot, partner_device, pair_count):
    held, virtuals, columns = factors.shape
    pair_slots = i_slot.shape[0]
    occ_count = lax.axis_size("occ")
    aux_count = lax.axis_size("aux")
    orbitals = occ_energy.shape[0]
    me, part = lax.axis_index("occ"), lax.axis_index("aux")
    core = me % 2
    rows = held * virtuals
    share = rows // aux_count
    parts_per_orbital = virtuals // share
    slot_of_part = part // parts_per_orbital
    first_virtual = (part % parts_per_orbital) * share

    flat = factors.reshape(rows, columns)
    turned = lax.all_to_all(jnp.broadcast_to(flat, (aux_count, rows, columns)), "aux", 0, 0)
    mine = lax.dynamic_slice(turned, (0, part * share, 0), (aux_count, share, columns))
    mine = mine.transpose(1, 0, 2).reshape(share, -1)
    chunks, late = gathered(mine, share // 2)
    own = turned.transpose(1, 0, 2).reshape(rows, -1)
    owns = [own, shift(own, "core", 1)]

    living = jnp.arange(pair_slots, dtype=jnp.int32) < pair_count[0]
    target = partner_device[:, 0]
    own_hot = (i_slot[:, None] == jnp.arange(held, dtype=jnp.int32)[None, :]) & living[:, None]
    far_hot = target[:, None] == jnp.arange(occ_count, dtype=jnp.int32)[None, :]
    far_hot = far_hot & (j_slot == slot_of_part)[:, None]
    counts = jnp.sum((own_hot[:, :, None] & far_hot[:, None, :]).astype(jnp.int32), axis=0)
    sent = jnp.concatenate([counts, shift(counts, "core", 1), jnp.zeros((4, occ_count), jnp.int32)])
    column = np.arange(8)[None, :]
    wanted = np.where(column < 2 * held, np.arange(occ_count)[:, None] ^ (column // held), -1)
    wanted_slot = np.broadcast_to(column % held, wanted.shape)
    match = (target[:, None, None] == jnp.asarray(wanted, jnp.int32)[None]) & (
        j_slot[:, None, None] == jnp.asarray(wanted_slot, jnp.int32)[None]
    )
    match = match & ((i_slot == slot_of_part) & living)[:, None, None]
    to_chip = jnp.sum(match.astype(jnp.int32), axis=0)
    to_chip, _ = lax.optimization_barrier((to_chip, late))
    came = lax.all_to_all(to_chip, "occ", 0, 0, tiled=True)

    energy = lambda device: lax.dynamic_slice(occ_energy, (device * held,), (held,))
    row_of = lambda device: (vir_energy[None, :] - energy(device)[:, None]).reshape(rows, 1)
    rows_of = [row_of(me), row_of(me + 1 - 2 * core)]
    x, z = me // STRIDE["x"], me // STRIDE["z"] % GRID["z"]
    far_virtual = lax.dynamic_slice(vir_energy, (first_virtual,), (share,))

    def tables(pieces):
        places = np.concatenate([p.places for p in pieces]).astype(np.int32)
        home = (x - jnp.asarray(places[:, 0])) % GRID["x"] * STRIDE["x"]
        home = home + (z - jnp.asarray(places[:, 1])) % GRID["z"] * STRIDE["z"] + core
        orbital = home * held + slot_of_part
        hot = orbital[None, :] == jnp.arange(orbitals, dtype=jnp.int32)[:, None]
        place_hot = jnp.asarray(places[:, 2])[None, :] == jnp.arange(share, dtype=jnp.int32)[:, None]
        col = jnp.sum(jnp.where(place_hot, far_virtual[:, None], 0.0), axis=0)
        col = col - jnp.sum(jnp.where(hot, occ_energy[:, None], 0.0), axis=0)
        return col[None, :], home[None, :]

    total = None
    for pieces in chunks[:-1]:
        total = contract(owns, rows_of, pieces, tables, sent, came, total, 0, virtuals, columns)
    last = [
        contract(
            owns[h : h + 1],
            rows_of[h : h + 1],
            chunks[-1],
            tables,
            sent,
            came,
            total,
            h,
            virtuals,
            columns,
        )[0]
        for h in (0, 1)
    ]
    partial = last[0] + shift(last[1], "core", 1)
    gamma = jnp.sum(lax.all_to_all(partial, "aux", 0, 0), axis=0)
    rounded = gamma.astype(jnp.bfloat16)
    terms = lax.dot_general(
        own, rounded, (((0,), (0,)), ((), ())), preferred_element_type=jnp.float32
    )
    terms = terms.reshape(occ_count // 2, 2, -1, columns)
    kept = lax.dynamic_index_in_dim(terms, core, axis=1, keepdims=False)
    given = lax.dynamic_index_in_dim(terms, 1 - core, axis=1, keepdims=False)
    kept = kept + shift(given, "core", 1)
    groups = [[2 * i + c for i in range(occ_count // 2)] for c in range(2)]
    spread = lax.all_to_all(kept, "occ", 0, 0, axis_index_groups=groups)
    total = jnp.sum(spread, axis=0)
    scale = 2.0 * float(orbitals * virtuals) ** (-0.5)
    return gamma.reshape(held, virtuals, columns), total.T * scale


def solution(mesh):
    placed = (P("occ", None, "aux"), P(), P(), P("occ"), P("occ"), P("occ", None), P("occ"))
    return jax.shard_map(
        body,
        mesh=mesh,
        in_specs=placed,
        out_specs=(P("occ", None, "aux"), P("aux", "occ")),
        check_vma=False,
    )
```

```python
import functools

import jax
import jax.numpy as jnp
import numpy as np
from jax import lax
from jax.experimental import pallas as pl
from jax.experimental.pallas import tpu as pltpu
from jax.sharding import PartitionSpec as P


GRID = {"x": 4, "z": 8, "core": 2}
STRIDE = {"x": 16, "z": 2, "core": 1}


def shift(value, axis, step):
    size, stride = GRID[axis], STRIDE[axis]
    pairs = []
    for index in range(64):
        at = index // stride % size
        pairs.append((index, index + ((at + step) % size - at) * stride))
    return lax.ppermute(value, "occ", pairs)


class Rows:
    def __init__(self, value, places):
        self.value, self.places = value, places

    def moved(self, axis, step):
        dx, dz = (step, 0) if axis == "x" else (0, step)
        return Rows(shift(self.value, axis, step), self.places + np.array([dx, dz, 0]))

    def part(self, start, stop):
        return Rows(self.value[start:stop], self.places[start:stop])


def joined(pieces):
    return Rows(
        jnp.concatenate([p.value for p in pieces], axis=0),
        np.concatenate([p.places for p in pieces], axis=0),
    )


def gathered(mine, half):
    share = mine.shape[0]
    places = np.stack([np.zeros(share, int), np.zeros(share, int), np.arange(share)], axis=1)
    whole = Rows(mine, places)
    a, b = whole.part(0, half), whole.part(half, share)
    ap, am = a.moved("z", 1), a.moved("z", -1)
    bp, bm = b.moved("x", 1), b.moved("x", -1)
    ap2, am2 = ap.moved("z", 1), am.moved("z", -1)
    b2 = bp.moved("x", 1)
    bb = joined([b, bp, bm, b2])
    a1 = joined([a, ap, am, ap2, am2])
    bz1, bzm1 = bb.moved("z", 1), bb.moved("z", -1)
    ap3, am3 = ap2.moved("z", 1), am2.moved("z", -1)
    ax1, axm1 = a1.moved("x", 1), a1.moved("x", -1)
    am4 = am3.moved("z", -1)
    bz2, bzm2 = bz1.moved("z", 1), bzm1.moved("z", -1)
    ax2 = ax1.moved("x", 1)
    a2 = joined([ap3, am3, am4])
    bz3, bzm3 = bz2.moved("z", 1), bzm2.moved("z", -1)
    cx1, cxm1 = a2.moved("x", 1), a2.moved("x", -1)
    bz4 = bz3.moved("z", 1)
    cxm2 = cxm1.moved("x", -1)
    return [
        [bb, a1, bz1, bzm1, ax1, axm1, ap3],
        [am3, ax2, bz2, bzm2, bz3, bzm3, cx1, cxm1],
        [am4, bz4, cxm2],
    ], ap.value, ap2.value


def pair_block(virtuals, sizes, halves, base, first, tile, *refs):
    count = len(sizes)
    own_refs, refs = refs[:halves], refs[halves:]
    row_refs, refs = refs[:halves], refs[halves:]
    (col_ref, home_ref, sent_ref, came_ref), refs = refs[:4], refs[4:]
    piece_refs, refs = refs[:count], refs[count:]
    before_ref, refs = (None, refs) if first else (refs[0], refs[1:])
    out_ref, far, amplitude, weight, total, piece_sem, before_sem, out_sem = refs
    fetches, start = [], 0
    for n, size in enumerate(sizes):
        copy = pltpu.make_async_copy(piece_refs[n], far.at[pl.ds(start, size)], piece_sem.at[n])
        copy.start()
        fetches.append(copy)
        start += size
    if not first:
        load = pltpu.make_async_copy(before_ref.at[pl.ds(base, halves)], total, before_sem)
        load.start()
    devices = came_ref.shape[0]
    hot = lax.broadcasted_iota(jnp.int32, (devices, start), 0) == home_ref[...]
    hot = jnp.where(hot, 1.0, 0.0).astype(jnp.bfloat16)
    narrow = lambda ref: ref[...].astype(jnp.float32).astype(jnp.bfloat16)
    weight[...] = jnp.dot(narrow(sent_ref), hot, preferred_element_type=jnp.float32) + lax.dot_general(
        narrow(came_ref), hot, (((0,), (0,)), ((), ())), preferred_element_type=jnp.float32
    )
    for copy in fetches:
        copy.wait()
    held = own_refs[0].shape[0] // virtuals
    blocks, width = total.shape[1], total.shape[3]
    stores = []
    for h in range(halves):

        def meet(span):
            x = lax.dot_general(
                own_refs[h][...],
                far[span, :],
                (((1,), (1,)), ((), ())),
                preferred_element_type=jnp.float32,
            )
            x = (x / (row_refs[h][...] + col_ref[:, span])).astype(jnp.bfloat16)
            for k in range(held):
                rows = slice(k * virtuals, (k + 1) * virtuals)
                at = (base + h) * held + k
                amplitude[rows, span] = x[rows] * weight[at : at + 1, span].astype(jnp.bfloat16)

        def step(t, _):
            meet(pl.ds(pl.multiple_of(t * tile, tile), tile))
            return 0

        lax.fori_loop(0, start // tile, step, 0)
        if start % tile:
            meet(pl.ds(start // tile * tile, start % tile))
        if h == 0 and not first:
            load.wait()

        def gain(q, _):
            span = pl.ds(pl.multiple_of(q * width, width), width)
            y = jnp.dot(amplitude[...], far[:, span], preferred_element_type=jnp.float32)
            total[h, q] = y if first else total[h, q] + y
            return 0

        lax.fori_loop(0, blocks, gain, 0)
        store = pltpu.make_async_copy(total.at[h], out_ref.at[h], out_sem.at[h])
        store.start()
        stores.append(store)
    for store in stores:
        store.wait()


def contract(owns, rows_of, pieces, tables, sent, came, before, base, virtuals, columns):
    rows, width = owns[0].shape
    sizes = tuple(p.value.shape[0] for p in pieces)
    far_rows = sum(sizes)
    halves = len(owns)
    first = before is None
    vmem = pl.BlockSpec(memory_space=pltpu.VMEM)
    anywhere = pl.BlockSpec(memory_space=pl.ANY)
    shape = (halves, width // columns, rows, columns)
    col, home = tables(pieces)
    operands = [*owns, *rows_of, col, home, sent, came, *[p.value for p in pieces]]
    in_specs = [vmem] * (2 * halves + 4) + [anywhere] * len(pieces)
    if not first:
        operands.append(before)
        in_specs.append(anywhere)
    return pl.pallas_call(
        functools.partial(pair_block, virtuals, sizes, halves, base, first, 256),
        out_shape=jax.ShapeDtypeStruct(shape, jnp.float32),
        in_specs=in_specs,
        out_specs=anywhere,
        scratch_shapes=[
            pltpu.VMEM((far_rows, width), jnp.bfloat16),
            pltpu.VMEM((rows, far_rows), jnp.bfloat16),
            pltpu.VMEM((sent.shape[0], far_rows), jnp.float32),
            pltpu.VMEM(shape, jnp.float32),
            pltpu.SemaphoreType.DMA((len(pieces),)),
            pltpu.SemaphoreType.DMA,
            pltpu.SemaphoreType.DMA((halves,)),
        ],
        compiler_params=pltpu.CompilerParams(vmem_limit_bytes=28 << 20),
        cost_estimate=pl.CostEstimate(
            flops=4 * halves * rows * far_rows * width,
            bytes_accessed=2 * far_rows * width + 8 * halves * rows * width,
            transcendentals=0,
        ),
        name="pair_block",
    )(*operands)


def body(factors, occ_energy, vir_energy, i_slot, j_slot, partner_device, pair_count):
    held, virtuals, columns = factors.shape
    pair_slots = i_slot.shape[0]
    occ_count = lax.axis_size("occ")
    aux_count = lax.axis_size("aux")
    orbitals = occ_energy.shape[0]
    me, part = lax.axis_index("occ"), lax.axis_index("aux")
    core = me % 2
    rows = held * virtuals
    share = rows // aux_count
    parts_per_orbital = virtuals // share
    slot_of_part = part // parts_per_orbital
    first_virtual = (part % parts_per_orbital) * share

    flat = factors.reshape(rows, columns)
    mine = lax.all_to_all(flat.reshape(aux_count, share, columns), "aux", 0, 0)
    mine = mine.transpose(1, 0, 2).reshape(share, -1)
    chunks, early, late = gathered(mine, share // 2)
    spread, _ = lax.optimization_barrier((flat, early))
    turned = lax.all_to_all(jnp.broadcast_to(spread, (aux_count, rows, columns)), "aux", 0, 0)
    own = turned.transpose(1, 0, 2).reshape(rows, -1)
    owns = [own, shift(own, "core", 1)]

    living = jnp.arange(pair_slots, dtype=jnp.int32) < pair_count[0]
    target = partner_device[:, 0]
    own_hot = (i_slot[:, None] == jnp.arange(held, dtype=jnp.int32)[None, :]) & living[:, None]
    far_hot = target[:, None] == jnp.arange(occ_count, dtype=jnp.int32)[None, :]
    far_hot = far_hot & (j_slot == slot_of_part)[:, None]
    counts = jnp.sum((own_hot[:, :, None] & far_hot[:, None, :]).astype(jnp.int32), axis=0)
    sent = jnp.concatenate([counts, shift(counts, "core", 1), jnp.zeros((4, occ_count), jnp.int32)])
    column = np.arange(8)[None, :]
    wanted = np.where(column < 2 * held, np.arange(occ_count)[:, None] ^ (column // held), -1)
    wanted_slot = np.broadcast_to(column % held, wanted.shape)
    match = (target[:, None, None] == jnp.asarray(wanted, jnp.int32)[None]) & (
        j_slot[:, None, None] == jnp.asarray(wanted_slot, jnp.int32)[None]
    )
    match = match & ((i_slot == slot_of_part) & living)[:, None, None]
    to_chip = jnp.sum(match.astype(jnp.int32), axis=0)
    to_chip, _ = lax.optimization_barrier((to_chip, late))
    came = lax.all_to_all(to_chip, "occ", 0, 0, tiled=True)

    energy = lambda device: lax.dynamic_slice(occ_energy, (device * held,), (held,))
    row_of = lambda device: (vir_energy[None, :] - energy(device)[:, None]).reshape(rows, 1)
    rows_of = [row_of(me), row_of(me + 1 - 2 * core)]
    x, z = me // STRIDE["x"], me // STRIDE["z"] % GRID["z"]
    far_virtual = lax.dynamic_slice(vir_energy, (first_virtual,), (share,))

    def tables(pieces):
        places = np.concatenate([p.places for p in pieces]).astype(np.int32)
        home = (x - jnp.asarray(places[:, 0])) % GRID["x"] * STRIDE["x"]
        home = home + (z - jnp.asarray(places[:, 1])) % GRID["z"] * STRIDE["z"] + core
        orbital = home * held + slot_of_part
        hot = orbital[None, :] == jnp.arange(orbitals, dtype=jnp.int32)[:, None]
        place_hot = jnp.asarray(places[:, 2])[None, :] == jnp.arange(share, dtype=jnp.int32)[:, None]
        col = jnp.sum(jnp.where(place_hot, far_virtual[:, None], 0.0), axis=0)
        col = col - jnp.sum(jnp.where(hot, occ_energy[:, None], 0.0), axis=0)
        return col[None, :], home[None, :]

    total = None
    for pieces in chunks[:-1]:
        total = contract(owns, rows_of, pieces, tables, sent, came, total, 0, virtuals, columns)
    last = [
        contract(
            owns[h : h + 1],
            rows_of[h : h + 1],
            chunks[-1],
            tables,
            sent,
            came,
            total,
            h,
            virtuals,
            columns,
        )[0]
        for h in (0, 1)
    ]
    partial = last[0] + shift(last[1], "core", 1)
    gamma = jnp.sum(lax.all_to_all(partial, "aux", 0, 0), axis=0)
    rounded = gamma.astype(jnp.bfloat16)
    terms = lax.dot_general(
        own, rounded, (((0,), (0,)), ((), ())), preferred_element_type=jnp.float32
    )
    terms = terms.reshape(occ_count // 2, 2, -1, columns)
    kept = lax.dynamic_index_in_dim(terms, core, axis=1, keepdims=False)
    given = lax.dynamic_index_in_dim(terms, 1 - core, axis=1, keepdims=False)
    kept = kept + shift(given, "core", 1)
    groups = [[2 * i + c for i in range(occ_count // 2)] for c in range(2)]
    spread = lax.all_to_all(kept, "occ", 0, 0, axis_index_groups=groups)
    total = jnp.sum(spread, axis=0)
    scale = 2.0 * float(orbitals * virtuals) ** (-0.5)
    return gamma.reshape(held, virtuals, columns), total.T * scale


def solution(mesh):
    placed = (P("occ", None, "aux"), P(), P(), P("occ"), P("occ"), P("occ", None), P("occ"))
    return jax.shard_map(
        body,
        mesh=mesh,
        in_specs=placed,
        out_specs=(P("occ", None, "aux"), P("aux", "occ")),
        check_vma=False,
    )
```
